32 devices in a mesh: row: 4 (over y, x), col: 8 (over z, core).
Axes of the slice: x: 2, y: 2, z: 4, core: 2. Of those that a mesh axis runs over, the one named last changes fastest.
Arguments:
- activations: bfloat16 [512, 16384], P('col', 'row'), may hold values from -6 to 6
- grad_output: bfloat16 [512, 16384], P('col', 'row'), may hold values from -6 to 6
- gate_pre: bfloat16 [512, 8192], P('row', 'col'), may hold values from -8 to 8
- up_pre: bfloat16 [512, 8192], P('row', 'col'), may hold values from -6 to 6
- w_gate: bfloat16 [16384, 8192], P('row', 'col'), may hold values from -0.046875 to 0.046875
- w_up: bfloat16 [16384, 8192], P('row', 'col'), may hold values from -0.046875 to 0.046875
- w_down: bfloat16 [8192, 16384], P('col', 'row'), may hold values from -0.0625 to 0.0625
Outputs:
- grad_input: bfloat16 [512, 16384], P('col', 'row')
- grad_gate: bfloat16 [16384, 8192], P('row', 'col')
- grad_up: bfloat16 [16384, 8192], P('row', 'col')
- grad_down: bfloat16 [8192, 16384], P('col', 'row')
The draws below stay inside these ranges and needn't reach their ends.
All inputs are finite; a program needn't handle non-finite values.
Results may differ from the reference program's by a relative error of at most 0.005.
Values may be sent and summed in bfloat16 or wider, within the bound.
A program may use at most 128 MiB of HBM per device.

```python
import jax
import jax.numpy as jnp
from jax import lax

D = 16384
FF = 8192
TOKENS = 512


def block_scale(rng, dims, pieces, low, largest):
    gain = 1.0
    for axis_at, blocks in pieces:
        draws = jax.random.uniform(jax.random.fold_in(jax.random.fold_in(rng, 6), axis_at), (blocks,), jnp.float32, low / len(pieces), largest / len(pieces))
        gain = gain * jnp.repeat(jnp.exp(draws), dims[axis_at] // blocks).reshape((-1,) + (1,) * (len(dims) - 1 - axis_at))
    return gain


def normal_values(stream_key, shape, scale, reach, pieces=(), held_as=jnp.bfloat16):
    factor_of = block_scale(stream_key, shape, pieces, -0.22, 0.18) if pieces else 1.0
    values = jax.random.normal(stream_key, shape, jnp.float32) * scale * factor_of
    return jnp.minimum(jnp.maximum(values, -reach), reach).astype(held_as)


def setup_inputs(seed: int = 0) -> dict:
    splits = jax.random.split(jax.random.key(seed), 8)
    return {
        "activations": normal_values(splits[0], (TOKENS, D), 1.0, 6.0, ((0, 8), (1, 4))),
        "grad_output": normal_values(splits[1], (TOKENS, D), 1.0, 6.0, ((0, 8), (1, 4))),
        "gate_pre": normal_values(splits[2], (TOKENS, FF), 1.5, 8.0, ((0, 4), (1, 8))),
        "up_pre": normal_values(splits[3], (TOKENS, FF), 1.0, 6.0, ((0, 4), (1, 8))),
        "w_gate": normal_values(splits[4], (D, FF), D ** -0.5, 0.046875, ((0, 4), (1, 8))),
        "w_up": normal_values(splits[5], (D, FF), D ** -0.5, 0.046875, ((0, 4), (1, 8))),
        "w_down": normal_values(splits[6], (FF, D), FF ** -0.5, 0.0625, ((0, 8), (1, 4))),
    }


def reference(activations, grad_output, gate_pre, up_pre, w_gate, w_up, w_down):
    gate_val = gate_pre.astype(jnp.float32)
    up_val = up_pre.astype(jnp.float32)
    sigma = 1.0 / (1.0 + jnp.exp(-gate_val))
    hidden = (gate_val * sigma * up_val).astype(jnp.bfloat16)
    grad_hidden = lax.dot_general(grad_output, w_down, (((1,), (1,)), ((), ())), preferred_element_type=jnp.float32)
    grad_gate_pre = (grad_hidden * up_val * sigma * (1.0 + gate_val * (1.0 - sigma))).astype(jnp.bfloat16)
    grad_up_pre = (grad_hidden * gate_val * sigma).astype(jnp.bfloat16)
    contract_rows = (((0,), (0,)), ((), ()))
    grad_down = lax.dot_general(hidden, grad_output, contract_rows, preferred_element_type=jnp.float32).astype(jnp.bfloat16)
    grad_gate = lax.dot_general(activations, grad_gate_pre, contract_rows, preferred_element_type=jnp.float32).astype(jnp.bfloat16)
    grad_up = lax.dot_general(activations, grad_up_pre, contract_rows, preferred_element_type=jnp.float32).astype(jnp.bfloat16)
    contract_cols = (((1,), (1,)), ((), ()))
    grad_input = lax.dot_general(grad_gate_pre, w_gate, contract_cols, preferred_element_type=jnp.float32)
    grad_input = grad_input + lax.dot_general(grad_up_pre, w_up, contract_cols, preferred_element_type=jnp.float32)
    return grad_input.astype(jnp.bfloat16), grad_gate, grad_up, grad_down
```

```python
import functools

import jax
import jax.numpy as jnp
from jax import lax
from jax.experimental import pallas as pl
from jax.experimental.pallas import tpu as pltpu
from jax.sharding import PartitionSpec as P


CONTRACT_COLS = (((1,), (1,)), ((), ()))
CONTRACT_ROWS = (((0,), (0,)), ((), ()))
F32 = jnp.float32
BF16 = jnp.bfloat16


def tile_of(size, want):
    tile = min(size, want)
    while size % tile:
        tile //= 2
    return tile


def outer_kernel(lhs_ref, *refs):
    count = len(refs) // 2
    lhs = lhs_ref[...]
    for rhs_ref, out_ref in zip(refs[:count], refs[count:]):
        out_ref[...] = lax.dot_general(
            lhs, rhs_ref[...], CONTRACT_ROWS, preferred_element_type=F32
        ).astype(out_ref.dtype)


def token_sum(lhs, *rhs):
    tokens, rows = lhs.shape
    cols = rhs[0].shape[1]
    tile = tile_of(rows, 512)
    count = len(rhs)
    return pl.pallas_call(
        outer_kernel,
        grid=(rows // tile,),
        in_specs=[pl.BlockSpec((tokens, tile), lambda i: (0, i))]
        + [pl.BlockSpec((tokens, cols), lambda i: (0, 0))] * count,
        out_specs=[pl.BlockSpec((tile, cols), lambda i: (i, 0))] * count,
        out_shape=[jax.ShapeDtypeStruct((rows, cols), BF16)] * count,
        cost_estimate=pl.CostEstimate(
            flops=2 * tokens * rows * cols * count,
            bytes_accessed=2 * (tokens * rows + count * (tokens + rows) * cols),
            transcendentals=0,
        ),
        name="token_sum",
    )(lhs, *rhs)


def local(row_size, col_size, activations, grad_output, gate_pre, up_pre, w_gate, w_up, w_down):
    chips = col_size // 2
    row = lax.axis_index("row")
    col = lax.axis_index("col")
    chip, core = col // 2, col % 2
    shard = activations.shape[0]
    tokens = shard * col_size
    width = activations.shape[1]
    rows = gate_pre.shape[0]
    pair = [(i, i ^ 1) for i in range(col_size)]
    ring = [(i, (i + 2) % col_size) for i in range(col_size)]
    power = row_size & (row_size - 1) == 0

    def row_peer(index, step):
        return index ^ step if power else (index + step) % row_size

    def row_source(index, step):
        return index ^ step if power else (index - step) % row_size

    def row_perm(step):
        return [(i, row_peer(i, step)) for i in range(row_size)]

    def ring_gather(part):
        own = part
        for step in range(chips):
            after = lax.ppermute(own, "col", ring) if step < chips - 1 else None
            other = lax.ppermute(own, "col", pair)
            source = (chip - step) % chips
            yield source, own, other
            own = after

    def place(whole, source, own, other):
        whole = lax.dynamic_update_slice(whole, own, ((source * 2 + core) * shard, 0))
        return lax.dynamic_update_slice(whole, other, ((source * 2 + 1 - core) * shard, 0))

    def row_gather(part):
        whole = jnp.zeros((tokens, part.shape[1]), part.dtype)
        whole = lax.dynamic_update_slice(whole, part, (row * rows, 0))
        for step in range(1, row_size):
            got = lax.ppermute(part, "row", row_perm(step))
            whole = lax.dynamic_update_slice(whole, got, (row_source(row, step) * rows, 0))
        return whole

    gate_val = gate_pre.astype(F32)
    up_val = up_pre.astype(F32)
    sigma = 1.0 / (1.0 + jnp.exp(-gate_val))
    hidden = (gate_val * sigma * up_val).astype(BF16)

    grad_whole = jnp.zeros((tokens, width), BF16)
    partial = jnp.zeros((tokens, w_down.shape[0]), F32)
    for source, own, other in ring_gather(grad_output):
        grad_whole = place(grad_whole, source, own, other)
        last_own = own
        both = jnp.where(
            core == 0, jnp.concatenate([own, other]), jnp.concatenate([other, own])
        )
        product = lax.dot_general(both, w_down, CONTRACT_COLS, preferred_element_type=F32)
        partial = lax.dynamic_update_slice(
            partial, product, (source * 2 * shard, 0)
        )

    hidden_all = row_gather(hidden)

    def row_slice(index):
        return lax.dynamic_slice_in_dim(partial, index * rows, rows)

    grad_hidden = row_slice(row)
    for step in range(1, row_size):
        grad_hidden = grad_hidden + lax.ppermute(
            row_slice(row_peer(row, step)).astype(BF16), "row", row_perm(step)
        ).astype(F32)
    acts_own = [lax.optimization_barrier((activations, last_own))[0]]

    def acts_hop(held):
        if len(acts_own) == chips:
            return held
        held, got = lax.optimization_barrier(
            (held, lax.ppermute(acts_own[-1], "col", ring))
        )
        acts_own.append(got)
        return held

    grad_hidden = acts_hop(grad_hidden)
    grad_gate_pre = (
        grad_hidden * up_val * sigma * (1.0 + gate_val * (1.0 - sigma))
    ).astype(BF16)
    grad_up_pre = (grad_hidden * gate_val * sigma).astype(BF16)

    gate_grad_all = acts_hop(row_gather(grad_gate_pre))
    up_grad_all = acts_hop(row_gather(grad_up_pre))
    while len(acts_own) < chips:
        acts_hop(up_grad_all)

    acts_whole = jnp.zeros((tokens, width), BF16)
    for step, own in enumerate(acts_own):
        other = lax.ppermute(own, "col", pair)
        acts_whole = place(acts_whole, (chip - step) % chips, own, other)

    def product(grads, weights, index):
        return lax.dot_general(
            lax.dynamic_slice_in_dim(grads, index * 2 * shard, 2 * shard),
            weights,
            CONTRACT_COLS,
            preferred_element_type=F32,
        )

    (grad_down,) = token_sum(hidden_all, grad_whole)
    (grad_gate,) = token_sum(acts_whole, gate_grad_all)
    (grad_up,) = token_sum(acts_whole, up_grad_all)

    arrived = None
    for step in range(chips):
        index = (chip - 1 - step) % chips
        total = product(gate_grad_all, w_gate, index) + product(up_grad_all, w_up, index)
        mine = lax.dynamic_slice_in_dim(total, core * shard, shard)
        theirs = lax.dynamic_slice_in_dim(total, (1 - core) * shard, shard).astype(BF16)
        summed = mine + lax.ppermute(theirs, "col", pair).astype(F32)
        if arrived is not None:
            summed = summed + arrived.astype(F32)
        if step < chips - 1:
            sent = summed.astype(BF16)
            if step == 0:
                later, sent = lax.optimization_barrier((up_grad_all, sent))
            arrived = lax.ppermute(sent, "col", ring)
            if step == chips - 3:
                arrived, grad_gate = lax.optimization_barrier((arrived, grad_gate))
        if step == 1 and chips > 2:
            up_grad_all = later
    grad_input = summed.astype(BF16)
    return (grad_input, grad_gate, grad_up, grad_down)


def solution(mesh):
    in_specs = (
        P("col", "row"),
        P("col", "row"),
        P("row", "col"),
        P("row", "col"),
        P("row", "col"),
        P("row", "col"),
        P("col", "row"),
    )
    out_specs = (P("col", "row"), P("row", "col"), P("row", "col"), P("col", "row"))
    body = functools.partial(local, mesh.shape["row"], mesh.shape["col"])
    return jax.shard_map(body, mesh=mesh, in_specs=in_specs, out_specs=out_specs, check_vma=False)
```

```python
import functools

import jax
import jax.numpy as jnp
from jax import lax
from jax.experimental import pallas as pl
from jax.experimental.pallas import tpu as pltpu
from jax.sharding import PartitionSpec as P


CONTRACT_COLS = (((1,), (1,)), ((), ()))
CONTRACT_ROWS = (((0,), (0,)), ((), ()))
F32 = jnp.float32
BF16 = jnp.bfloat16


def tile_of(size, want):
    tile = min(size, want)
    while size % tile:
        tile //= 2
    return tile


def outer_kernel(lhs_ref, *refs):
    count = len(refs) // 2
    lhs = lhs_ref[...]
    for rhs_ref, out_ref in zip(refs[:count], refs[count:]):
        out_ref[...] = lax.dot_general(
            lhs, rhs_ref[...], CONTRACT_ROWS, preferred_element_type=F32
        ).astype(out_ref.dtype)


def token_sum(lhs, *rhs):
    tokens, rows = lhs.shape
    cols = rhs[0].shape[1]
    tile = tile_of(rows, 512)
    count = len(rhs)
    return pl.pallas_call(
        outer_kernel,
        grid=(rows // tile,),
        in_specs=[pl.BlockSpec((tokens, tile), lambda i: (0, i))]
        + [pl.BlockSpec((tokens, cols), lambda i: (0, 0))] * count,
        out_specs=[pl.BlockSpec((tile, cols), lambda i: (i, 0))] * count,
        out_shape=[jax.ShapeDtypeStruct((rows, cols), BF16)] * count,
        cost_estimate=pl.CostEstimate(
            flops=2 * tokens * rows * cols * count,
            bytes_accessed=2 * (tokens * rows + count * (tokens + rows) * cols),
            transcendentals=0,
        ),
        name="token_sum",
    )(lhs, *rhs)


def parts_kernel(count, starts_ref, *refs):
    whole = refs[-1]
    for i, part in enumerate(refs[:count]):
        size = part.shape[0]
        whole[pl.ds(pl.multiple_of(starts_ref[i], size), size), :] = part[...]
    rhs_ref, out_ref = refs[count : count + 2]
    out_ref[...] = lax.dot_general(
        whole[...], rhs_ref[...], CONTRACT_ROWS, preferred_element_type=F32
    ).astype(out_ref.dtype)


def parts_sum(starts, parts, rhs):
    tokens, cols = rhs.shape
    shard, rows = parts[0].shape
    tile = tile_of(rows, 512)
    count = len(parts)
    return pl.pallas_call(
        functools.partial(parts_kernel, count),
        grid_spec=pltpu.PrefetchScalarGridSpec(
            num_scalar_prefetch=1,
            grid=(rows // tile,),
            in_specs=[pl.BlockSpec((shard, tile), lambda i, starts: (0, i))] * count
            + [pl.BlockSpec((tokens, cols), lambda i, starts: (0, 0))],
            out_specs=pl.BlockSpec((tile, cols), lambda i, starts: (i, 0)),
            scratch_shapes=[pltpu.VMEM((tokens, tile), BF16)],
        ),
        out_shape=jax.ShapeDtypeStruct((rows, cols), BF16),
        cost_estimate=pl.CostEstimate(
            flops=2 * tokens * rows * cols,
            bytes_accessed=2 * (tokens * rows + (tokens + rows) * cols),
            transcendentals=0,
        ),
        name="parts_sum",
    )(starts, *parts, rhs)


def local(row_size, col_size, activations, grad_output, gate_pre, up_pre, w_gate, w_up, w_down):
    chips = col_size // 2
    row = lax.axis_index("row")
    col = lax.axis_index("col")
    chip, core = col // 2, col % 2
    shard = activations.shape[0]
    tokens = shard * col_size
    width = activations.shape[1]
    rows = gate_pre.shape[0]
    pair = [(i, i ^ 1) for i in range(col_size)]
    power = row_size & (row_size - 1) == 0

    def hop(step):
        return [(i, (i + 2 * step) % col_size) for i in range(col_size)]

    ring = hop(1)

    def row_peer(index, step):
        return index ^ step if power else (index + step) % row_size

    def row_source(index, step):
        return index ^ step if power else (index - step) % row_size

    def row_perm(step):
        return [(i, row_peer(i, step)) for i in range(row_size)]

    def ring_gather(part):
        own = part
        for step in range(chips):
            after = lax.ppermute(own, "col", ring) if step < chips - 1 else None
            other = lax.ppermute(own, "col", pair)
            source = (chip - step) % chips
            yield source, own, other
            own = after

    def place(whole, source, own, other):
        whole = lax.dynamic_update_slice(whole, own, ((source * 2 + core) * shard, 0))
        return lax.dynamic_update_slice(whole, other, ((source * 2 + 1 - core) * shard, 0))

    def row_gather(part):
        whole = jnp.zeros((tokens, part.shape[1]), part.dtype)
        whole = lax.dynamic_update_slice(whole, part, (row * rows, 0))
        for step in range(1, row_size):
            got = lax.ppermute(part, "row", row_perm(step))
            whole = lax.dynamic_update_slice(whole, got, (row_source(row, step) * rows, 0))
        return whole

    gate_val = gate_pre.astype(F32)
    up_val = up_pre.astype(F32)
    sigma = 1.0 / (1.0 + jnp.exp(-gate_val))
    hidden = (gate_val * sigma * up_val).astype(BF16)

    grad_whole = jnp.zeros((tokens, width), BF16)
    partial = jnp.zeros((tokens, w_down.shape[0]), F32)
    for source, own, other in ring_gather(grad_output):
        grad_whole = place(grad_whole, source, own, other)
        last_own = own
        both = jnp.where(
            core == 0, jnp.concatenate([own, other]), jnp.concatenate([other, own])
        )
        product = lax.dot_general(both, w_down, CONTRACT_COLS, preferred_element_type=F32)
        partial = lax.dynamic_update_slice(
            partial, product, (source * 2 * shard, 0)
        )

    hidden_all = row_gather(hidden)

    def row_slice(index):
        return lax.dynamic_slice_in_dim(partial, index * rows, rows)

    grad_hidden = row_slice(row)
    for step in range(1, row_size):
        grad_hidden = grad_hidden + lax.ppermute(
            row_slice(row_peer(row, step)).astype(BF16), "row", row_perm(step)
        ).astype(F32)
    activations, _ = lax.optimization_barrier((activations, last_own))
    acts_own = [activations] + [
        lax.ppermute(activations, "col", hop(step)) for step in range(1, chips)
    ]
    (grad_down,) = token_sum(hidden_all, grad_whole)
    grad_hidden, grad_down = lax.optimization_barrier((grad_hidden, grad_down))
    grad_gate_pre = (
        grad_hidden * up_val * sigma * (1.0 + gate_val * (1.0 - sigma))
    ).astype(BF16)
    grad_up_pre = (grad_hidden * gate_val * sigma).astype(BF16)

    gate_grad_all = row_gather(grad_gate_pre)
    up_grad_all = row_gather(grad_up_pre)

    starts = jnp.stack(
        [
            (((chip - step) % chips) * 2 + side) * shard
            for side in (core, 1 - core)
            for step in range(chips)
        ]
    ).astype(jnp.int32)

    def product(grads, weights, index):
        return lax.dot_general(
            lax.dynamic_slice_in_dim(grads, index * 2 * shard, 2 * shard),
            weights,
            CONTRACT_COLS,
            preferred_element_type=F32,
        )

    gate_step, up_step = min(1, chips - 2), min(2, chips - 2)
    arrived = None
    for step in range(chips):
        index = (chip - 1 - step) % chips
        total = product(gate_grad_all, w_gate, index) + product(up_grad_all, w_up, index)
        mine = lax.dynamic_slice_in_dim(total, core * shard, shard)
        theirs = lax.dynamic_slice_in_dim(total, (1 - core) * shard, shard).astype(BF16)
        summed = mine + lax.ppermute(theirs, "col", pair).astype(F32)
        if arrived is not None:
            summed = summed + arrived.astype(F32)
        if step < chips - 1:
            sent = summed.astype(BF16)
            if step == 0:
                later, acts_own, sent = lax.optimization_barrier(
                    (up_grad_all, acts_own, sent)
                )
                acts_parts = acts_own + [lax.ppermute(own, "col", pair) for own in acts_own]
            if step == gate_step:
                acts_parts, sent = lax.optimization_barrier((acts_parts, sent))
                grad_gate = parts_sum(starts, acts_parts, gate_grad_all)
            if step == up_step:
                acts_parts, grad_gate, sent = lax.optimization_barrier(
                    (acts_parts, grad_gate, sent)
                )
                grad_up = parts_sum(starts, acts_parts, up_grad_all)
            arrived = lax.ppermute(sent, "col", ring)
        if step == 1 and chips > 2:
            up_grad_all = later
    grad_input = summed.astype(BF16)
    return (grad_input, grad_gate, grad_up, grad_down)


def solution(mesh):
    in_specs = (
        P("col", "row"),
        P("col", "row"),
        P("row", "col"),
        P("row", "col"),
        P("row", "col"),
        P("row", "col"),
        P("col", "row"),
    )
    out_specs = (P("col", "row"), P("row", "col"), P("row", "col"), P("col", "row"))
    body = functools.partial(local, mesh.shape["row"], mesh.shape["col"])
    return jax.shard_map(body, mesh=mesh, in_specs=in_specs, out_specs=out_specs, check_vma=False)
```

```python
import functools

import jax
import jax.numpy as jnp
from jax import lax
from jax.experimental import pallas as pl
from jax.experimental.pallas import tpu as pltpu
from jax.sharding import PartitionSpec as P


CONTRACT_COLS = (((1,), (1,)), ((), ()))
CONTRACT_ROWS = (((0,), (0,)), ((), ()))
F32 = jnp.float32
BF16 = jnp.bfloat16


def tile_of(size, want):
    tile = min(size, want)
    while size % tile:
        tile //= 2
    return tile


def gathered_kernel(count, starts_ref, lhs_ref, *refs):
    rhs_refs, out_ref, whole = refs[:count], refs[count], refs[count + 1]

    @pl.when(pl.program_id(0) == 0)
    def _():
        for i, part in enumerate(rhs_refs):
            size = part.shape[0]
            whole[pl.ds(pl.multiple_of(starts_ref[i], size), size), :] = part[...]

    out_ref[...] = lax.dot_general(
        lhs_ref[...], whole[...], CONTRACT_ROWS, preferred_element_type=F32
    ).astype(out_ref.dtype)


def gathered_sum(starts, lhs, parts):
    tokens, rows = lhs.shape
    shard, cols = parts[0].shape
    tile = tile_of(rows, 256)
    count = len(parts)
    return pl.pallas_call(
        functools.partial(gathered_kernel, count),
        grid_spec=pltpu.PrefetchScalarGridSpec(
            num_scalar_prefetch=1,
            grid=(rows // tile,),
            in_specs=[pl.BlockSpec((tokens, tile), lambda i, starts: (0, i))]
            + [pl.BlockSpec((shard, cols), lambda i, starts: (0, 0))] * count,
            out_specs=pl.BlockSpec((tile, cols), lambda i, starts: (i, 0)),
            scratch_shapes=[pltpu.VMEM((tokens, cols), BF16)],
        ),
        out_shape=jax.ShapeDtypeStruct((rows, cols), BF16),
        cost_estimate=pl.CostEstimate(
            flops=2 * tokens * rows * cols,
            bytes_accessed=2 * (tokens * rows + (tokens + rows) * cols),
            transcendentals=0,
        ),
        name="gathered_sum",
    )(starts, lhs, *parts)


def parts_kernel(count, starts_ref, *refs):
    whole = refs[-1]
    for i, part in enumerate(refs[:count]):
        size = part.shape[0]
        whole[pl.ds(pl.multiple_of(starts_ref[i], size), size), :] = part[...]
    rhs_ref, out_ref = refs[count : count + 2]
    out_ref[...] = lax.dot_general(
        whole[...], rhs_ref[...], CONTRACT_ROWS, preferred_element_type=F32
    ).astype(out_ref.dtype)


def parts_sum(starts, parts, rhs):
    tokens, cols = rhs.shape
    shard, rows = parts[0].shape
    tile = tile_of(rows, 512)
    count = len(parts)
    return pl.pallas_call(
        functools.partial(parts_kernel, count),
        grid_spec=pltpu.PrefetchScalarGridSpec(
            num_scalar_prefetch=1,
            grid=(rows // tile,),
            in_specs=[pl.BlockSpec((shard, tile), lambda i, starts: (0, i))] * count
            + [pl.BlockSpec((tokens, cols), lambda i, starts: (0, 0))],
            out_specs=pl.BlockSpec((tile, cols), lambda i, starts: (i, 0)),
            scratch_shapes=[pltpu.VMEM((tokens, tile), BF16)],
        ),
        out_shape=jax.ShapeDtypeStruct((rows, cols), BF16),
        cost_estimate=pl.CostEstimate(
            flops=2 * tokens * rows * cols,
            bytes_accessed=2 * (tokens * rows + (tokens + rows) * cols),
            transcendentals=0,
        ),
        name="parts_sum",
    )(starts, *parts, rhs)


def local(row_size, col_size, activations, grad_output, gate_pre, up_pre, w_gate, w_up, w_down):
    chips = col_size // 2
    row = lax.axis_index("row")
    col = lax.axis_index("col")
    chip, core = col // 2, col % 2
    shard = activations.shape[0]
    tokens = shard * col_size
    width = activations.shape[1]
    rows = gate_pre.shape[0]
    pair = [(i, i ^ 1) for i in range(col_size)]
    power = row_size & (row_size - 1) == 0

    def hop(step):
        return [(i, (i + 2 * step) % col_size) for i in range(col_size)]

    ring = hop(1)

    def row_peer(index, step):
        return index ^ step if power else (index + step) % row_size

    def row_source(index, step):
        return index ^ step if power else (index - step) % row_size

    def row_perm(step):
        return [(i, row_peer(i, step)) for i in range(row_size)]

    def ring_gather(part):
        own = part
        for step in range(chips):
            after = lax.ppermute(own, "col", ring) if step < chips - 1 else None
            other = lax.ppermute(own, "col", pair)
            source = (chip - step) % chips
            yield source, own, other
            own = after

    def row_gather(part):
        whole = jnp.zeros((tokens, part.shape[1]), part.dtype)
        whole = lax.dynamic_update_slice(whole, part, (row * rows, 0))
        for step in range(1, row_size):
            got = lax.ppermute(part, "row", row_perm(step))
            whole = lax.dynamic_update_slice(whole, got, (row_source(row, step) * rows, 0))
        return whole

    gate_val = gate_pre.astype(F32)
    up_val = up_pre.astype(F32)
    sigma = 1.0 / (1.0 + jnp.exp(-gate_val))
    hidden = (gate_val * sigma * up_val).astype(BF16)

    grad_own, grad_other = [], []
    partial = jnp.zeros((tokens, w_down.shape[0]), F32)
    for source, own, other in ring_gather(grad_output):
        grad_own.append(own)
        grad_other.append(other)
        both = jnp.where(
            core == 0, jnp.concatenate([own, other]), jnp.concatenate([other, own])
        )
        product = lax.dot_general(both, w_down, CONTRACT_COLS, preferred_element_type=F32)
        partial = lax.dynamic_update_slice(
            partial, product, (source * 2 * shard, 0)
        )

    starts = jnp.stack(
        [
            (((chip - step) % chips) * 2 + side) * shard
            for side in (core, 1 - core)
            for step in range(chips)
        ]
    ).astype(jnp.int32)

    hidden_all = row_gather(hidden)

    def row_slice(index):
        return lax.dynamic_slice_in_dim(partial, index * rows, rows)

    grad_hidden = row_slice(row)
    for step in range(1, row_size):
        piece = row_slice(row_peer(row, step)).astype(BF16)
        got = lax.ppermute(piece, "row", row_perm(step))
        grad_hidden = grad_hidden + got.astype(F32)
    activations, _ = lax.optimization_barrier((activations, grad_own[-1]))
    acts_own = [activations] + [
        lax.ppermute(activations, "col", hop(step)) for step in range(1, chips)
    ]
    grad_down = gathered_sum(starts, hidden_all, grad_own + grad_other)
    grad_hidden, grad_down = lax.optimization_barrier((grad_hidden, grad_down))
    grad_gate_pre = (
        grad_hidden * up_val * sigma * (1.0 + gate_val * (1.0 - sigma))
    ).astype(BF16)
    grad_up_pre = (grad_hidden * gate_val * sigma).astype(BF16)

    gate_grad_all = row_gather(grad_gate_pre)
    up_grad_all = row_gather(grad_up_pre)

    def product(grads, weights, index):
        return lax.dot_general(
            lax.dynamic_slice_in_dim(grads, index * 2 * shard, 2 * shard),
            weights,
            CONTRACT_COLS,
            preferred_element_type=F32,
        )

    gate_step, up_step = min(1, chips - 2), min(2, chips - 2)
    gate_total = lax.dot_general(
        gate_grad_all, w_gate, CONTRACT_COLS, preferred_element_type=F32
    )
    halves = [(0, width // 2), (width // 2, width - width // 2)]
    arrived = None
    for step in range(chips):
        index = (chip - 1 - step) % chips
        total = lax.dynamic_slice_in_dim(
            gate_total, index * 2 * shard, 2 * shard
        ) + product(up_grad_all, w_up, index)
        mine = lax.dynamic_slice_in_dim(total, core * shard, shard)
        theirs = lax.dynamic_slice_in_dim(total, (1 - core) * shard, shard).astype(BF16)
        other = lax.ppermute(theirs, "col", pair)
        summed = []
        for half, (low, size) in enumerate(halves):
            here = lax.slice_in_dim(mine, low, low + size, axis=1) + lax.slice_in_dim(
                other, low, low + size, axis=1
            ).astype(F32)
            if arrived is not None:
                here = here + arrived[half].astype(F32)
            if step < chips - 1:
                here = here.astype(BF16)
                mine, other, here = lax.optimization_barrier((mine, other, here))
            summed.append(here)
        if step < chips - 1:
            sent = summed
            if step == 0:
                later, acts_own, sent[-1] = lax.optimization_barrier(
                    (up_grad_all, acts_own, sent[-1])
                )
                acts_parts = acts_own + [lax.ppermute(own, "col", pair) for own in acts_own]
            if step == gate_step:
                acts_parts, sent[-1] = lax.optimization_barrier((acts_parts, sent[-1]))
                grad_gate = parts_sum(starts, acts_parts, gate_grad_all)
            if step == up_step:
                grad_gate, sent[0] = lax.optimization_barrier((grad_gate, sent[0]))
                acts_parts, sent[-1] = lax.optimization_barrier((acts_parts, sent[-1]))
                grad_up = parts_sum(starts, acts_parts, up_grad_all)
            arrived = [lax.ppermute(half, "col", ring) for half in sent]
        if step == 1 and chips > 2:
            up_grad_all = later
    grad_input = jnp.concatenate([half.astype(BF16) for half in summed], axis=1)
    return (grad_input, grad_gate, grad_up, grad_down)


def solution(mesh):
    in_specs = (
        P("col", "row"),
        P("col", "row"),
        P("row", "col"),
        P("row", "col"),
        P("row", "col"),
        P("row", "col"),
        P("col", "row"),
    )
    out_specs = (P("col", "row"), P("row", "col"), P("row", "col"), P("col", "row"))
    body = functools.partial(local, mesh.shape["row"], mesh.shape["col"])
    return jax.shard_map(body, mesh=mesh, in_specs=in_specs, out_specs=out_specs, check_vma=False)
```
